512 devices in a mesh: factor: 16 (over x_hi, y, core), load: 32 (over z, x_lo).
Axes of the slice: x: 4 (x_hi: 2, x_lo: 2; x = x_hi * 2 + x_lo), y: 4, z: 16, core: 2. Of those that a mesh axis runs over, the one named last changes fastest.
Arguments:
- b_panel: bfloat16 [2048, 8192], P('factor', 'load'), may hold values from -6 to 6
- b_update: bfloat16 [8192, 8192], P('factor', 'load'), may hold values from -6 to 6
- panel_inverse: bfloat16 [2048, 2048], P('factor'), as said below
- update_factor: bfloat16 [8192, 2048], P('factor'), may hold values from -0.125 to 0.125
- update_solution: bfloat16 [8192, 8192], P(('factor', 'load')), may hold values from -3 to 3
- axle_weights: bfloat16 [3072, 8192], P('load'), may hold values from -0.0625 to 0.0625
Outputs:
- update_rhs: bfloat16 [8192, 8192], P('factor', 'load')
- panel_solution: bfloat16 [2048, 8192], P('factor', 'load')
- config_response: float32 [3072, 2048], P('load', 'factor')
The draws below stay inside these ranges and needn't reach their ends.
Inputs may be any that keep to these rules, and one draw needn't show every extreme that they name: panel_inverse is zero above the diagonal and its diagonal lies between 1 and 2.
All inputs are finite; a program needn't handle non-finite values.
Results may differ from the reference program's by a relative error of at most 0.0052.
Values may be sent and summed in bfloat16 or wider, within the bound.
A program may use at most 64 MiB of HBM per device.

```python
import jax
import jax.numpy as jnp
from jax import lax

PANEL = 2048
UPD = 8192
CONFIGS = 3072
COLUMNS = 8192


def draw_panel_inverse(key, part):
    first, second = jax.random.split(jax.random.fold_in(key, 11))
    lower = jax.random.normal(first, (PANEL, PANEL), jnp.float32)
    lower = lower * (1.5 / PANEL ** 0.5)
    diagonal = jax.random.uniform(second, (PANEL,), jnp.float32, 1.0, 2.0)
    rows = jnp.arange(PANEL)[:, None]
    cols = jnp.arange(PANEL)[None, :]
    whole = jnp.where(rows > cols, lower, 0.0) + jnp.where(rows == cols, diagonal[None, :], 0.0)
    return whole.astype(jnp.bfloat16)


def level_of(key, shape, cuts, least, top_value):
    def one(axis_at, blocks):
        draws = jax.random.uniform(jax.random.fold_in(jax.random.fold_in(key, 6), axis_at), (blocks,), jnp.float32, least / len(cuts), top_value / len(cuts))
        return jnp.repeat(jnp.exp(draws), shape[axis_at] // blocks).reshape((-1,) + (1,) * (len(shape) - axis_at - 1))

    factor_of = one(*cuts[0])
    for cut in cuts[1:]:
        factor_of = factor_of * one(*cut)
    return factor_of


def gaussian(rng, extent, spread, reach, cuts=(), kind=jnp.bfloat16):
    values = jax.random.normal(rng, extent, jnp.float32) * spread
    if len(cuts) > 0:
        values = level_of(rng, extent, cuts, -0.22, 0.18) * values
    return jnp.clip(values, min=-reach, max=reach).astype(kind)


def setup_inputs(seed: int = 0) -> dict:
    splits = jax.random.split(jax.random.key(seed), 7)
    return {
        "b_panel": gaussian(splits[0], (PANEL, COLUMNS), 1.0, 6.0, ((0, 16), (1, 32))),
        "b_update": gaussian(splits[1], (UPD, COLUMNS), 1.0, 6.0, ((0, 16), (1, 32))),
        "panel_inverse": draw_panel_inverse(jax.random.fold_in(splits[6], 71), 0),
        "update_factor": gaussian(splits[3], (UPD, PANEL), PANEL ** -0.5, 0.125, ((0, 16),)),
        "update_solution": gaussian(splits[4], (UPD, COLUMNS), 0.5, 3.0, ((0, 512),)),
        "axle_weights": gaussian(splits[5], (CONFIGS, COLUMNS), COLUMNS ** -0.5, 0.0625, ((0, 32),)),
    }


def reference(b_panel, b_update, panel_inverse, update_factor, update_solution, axle_weights):
    forward = jnp.dot(panel_inverse, b_panel, preferred_element_type=jnp.float32).astype(jnp.bfloat16)
    lowered = jnp.dot(update_factor, forward, preferred_element_type=jnp.float32)
    update_rhs = (b_update.astype(jnp.float32) - lowered).astype(jnp.bfloat16)
    coupled = lax.dot_general(update_factor, update_solution, (((0,), (0,)), ((), ())), preferred_element_type=jnp.float32)
    reduced = (forward.astype(jnp.float32) - coupled).astype(jnp.bfloat16)
    panel_solution = lax.dot_general(panel_inverse, reduced, (((0,), (0,)), ((), ())), preferred_element_type=jnp.float32).astype(jnp.bfloat16)
    config_response = lax.dot_general(axle_weights, panel_solution, (((1,), (1,)), ((), ())), preferred_element_type=jnp.float32)
    return (update_rhs, panel_solution, config_response)
```

```python
import functools

import jax
import jax.numpy as jnp
from jax import lax
from jax.experimental import pallas as pl
from jax.experimental.pallas import tpu as pltpu
from jax.sharding import PartitionSpec as P

MESH = pl.DeviceIdType.MESH
BF16 = jnp.bfloat16
F32 = jnp.float32
CHIPS = 8
ROWS = 128
COLS = 256
PIECES = 2


def kernel(
    bp, bu, pinv, uf, xs, ws, out_u, out_s, out_r,
    bp_all, f_all, red_all, p_v, pc, pt, u_v, ut, x_r, bu_v, w2, s_all,
    c_out, c_in, c_own, rs_out, rs_in, r_acc, r_in,
    loc, x_s, x_rv, ag_s, ag_r, sib_s, sib_r, p_s, p_r, w_s, w_r, c_s, c_r, rs_s, rs_r, zs, zr, r_s,
):
    f = lax.axis_index("factor")
    l = lax.axis_index("load")
    j, c = f // 2, f % 2
    h, y = j // 4, j % 4
    z, s = l // 2, l % 2
    sib = 2 * j + 1 - c

    def rdma(src, dst, ss, rs, df, dl):
        return pltpu.make_async_remote_copy(
            src_ref=src, dst_ref=dst, send_sem=ss, recv_sem=rs,
            device_id={"factor": df, "load": dl}, device_id_type=MESH,
        )

    def rows(ref, i, n=ROWS):
        return ref.at[pl.ds(pl.multiple_of(i * n, n), n)]

    def cols(ref, i, n):
        return ref.at[:, pl.ds(pl.multiple_of(i * n, n), n)]

    l_u = pltpu.make_async_copy(uf, u_v, loc.at[0])
    l_p = pltpu.make_async_copy(pinv, p_v, loc.at[1])
    l_b = pltpu.make_async_copy(bp, rows(bp_all, f), loc.at[2])
    l_x = pltpu.make_async_copy(cols(xs, l, COLS), rows(x_r, l, 16), loc.at[3])
    l_bu = pltpu.make_async_copy(bu, bu_v, loc.at[4])
    l_pc = pltpu.make_async_copy(cols(pinv, f, ROWS), pc.at[f], loc.at[5])
    for cp in (l_b, l_p, l_x, l_u, l_bu, l_pc):
        cp.start()

    def l_w(i):
        return pltpu.make_async_copy(cols(ws, 2 * i + s, COLS), w2.at[i, pl.ds(0, 96)], loc.at[6 + i])

    @pl.loop(0, 16)
    def _(i):
        l_w(i).start()

    barrier = pltpu.get_barrier_semaphore()

    def hello(df, dl):
        pl.semaphore_signal(barrier, inc=1, device_id={"factor": df, "load": dl}, device_id_type=MESH)

    @pl.loop(1, 32)
    def _(d):
        hello(f, (l + d) % 32)

    @pl.loop(1, 8)
    def _(d):
        hello(h * 8 + (f + d) % 8, l)

    @pl.loop(0, 8)
    def _(d):
        hello((1 - h) * 8 + d, 2 * z + 1 - s)

    @pl.loop(0, 4)
    def _(d):
        hello((1 - h) * 8 + 2 * d + c, l)

    pl.semaphore_wait(barrier, 31 + 7 + 8 + 4)

    def chip_copy(k, buf, d, target):
        own = rows(buf, f)
        return rdma(own, own, ag_s.at[k, d], ag_r.at[k, d], 2 * ((j + d) % CHIPS) + c, l)

    def chip_recv(k, buf, d):
        got = rows(buf, 2 * ((j + CHIPS - d) % CHIPS) + c)
        return rdma(got, got, ag_s.at[k, d], ag_r.at[k, d], sib, l)

    def core_copy(k, buf, d):
        got = rows(buf, 2 * ((j + CHIPS - d) % CHIPS) + c)
        return rdma(got, got, sib_s.at[k, d], sib_r.at[k, d], sib, l)

    def gather_start(k, buf):
        @pl.loop(1, CHIPS)
        def _(d):
            chip_copy(k, buf, d, None).start()

        core_copy(k, buf, 0).start()

    def gather_forward(k, buf):
        @pl.loop(1, CHIPS)
        def _(d):
            chip_recv(k, buf, d).wait_recv()
            core_copy(k, buf, d).start()

    def gather_finish(k, buf):
        @pl.loop(0, CHIPS)
        def _(d):
            core_copy(k, buf, d).wait_recv()

    def gather_sent(k, buf):
        @pl.loop(1, CHIPS)
        def _(d):
            chip_copy(k, buf, d, None).wait_send()

        @pl.loop(0, CHIPS)
        def _(d):
            core_copy(k, buf, d).wait_send()

    def x_copy(d):
        to = (l + d) % 32
        return rdma(cols(xs, to, COLS), rows(x_r, l, 16), x_s.at[d], x_rv.at[d], f, to)

    def x_recv(d):
        got = rows(x_r, (l + 32 - d) % 32, 16)
        return rdma(got, got, x_s.at[d], x_rv.at[d], f, l)

    l_b.wait()
    gather_start(0, bp_all)

    @pl.loop(1, 32)
    def _(d):
        x_copy(d).start()

    def p_copy(d):
        to = (f + d) % 16
        same = 1 - (to // 8 + h) % 2
        dl = 2 * z + same * s + (1 - same) * (1 - s)
        return rdma(cols(p_v, to, ROWS), pc.at[f], p_s.at[d], p_r.at[d], to, dl)

    def p_recv(d):
        got = pc.at[(f + 16 - d) % 16]
        return rdma(got, got, p_s.at[d], p_r.at[d], sib, l)

    def w_copy(i):
        zz = 8 * c + i
        return rdma(
            cols(ws, 2 * zz + 1 - s, COLS), w2.at[zz, pl.ds(96, 96)], w_s.at[i], w_r.at[i], f, 2 * z + 1 - s
        )

    def w_core(i):
        got = w2.at[8 * c + i, pl.ds(96, 96)]
        return rdma(got, got, w_s.at[8 + i], w_r.at[8 + i], sib, l)

    def w_core_recv(i):
        got = w2.at[8 * (1 - c) + i, pl.ds(96, 96)]
        return rdma(got, got, w_s.at[8 + i], w_r.at[8 + i], sib, l)

    l_p.wait()
    gather_forward(0, bp_all)

    @pl.loop(1, 16)
    def _(d):
        p_copy(d).start()

    gather_finish(0, bp_all)
    fwd = jnp.dot(p_v[...], bp_all[...], preferred_element_type=F32).astype(BF16)
    f_all[pl.ds(pl.multiple_of(f * ROWS, ROWS), ROWS), :] = fwd
    gather_start(1, f_all)

    @pl.loop(0, 8)
    def _(i):
        w_copy(i).start()

    l_u.wait()

    @pl.loop(0, 16)
    def _(i):
        at = pl.ds(pl.multiple_of(i * ROWS, ROWS), ROWS)
        ut[at, :] = u_v[:, at].T

    gather_forward(1, f_all)

    l_x.wait()

    @pl.loop(1, 32)
    def _(d):
        x_recv(d).wait_recv()

    def c_copy(i):
        return rdma(c_out.at[i], c_in.at[i], c_s.at[i], c_r.at[i], sib, l)

    def partial(i, core):
        at = pl.ds(pl.multiple_of((2 * i + core) * ROWS, ROWS), ROWS)
        return jnp.dot(ut[at, :], x_r[...], preferred_element_type=F32)

    @pl.loop(0, CHIPS)
    def _(i):
        c_out[i] = partial(i, 1 - c).astype(BF16)
        c_copy(i).start()

    @pl.loop(0, CHIPS)
    def _(i):
        c_own[i] = partial(i, c)

    def rs_copy(d):
        to = (j + d) % CHIPS
        return rdma(rs_out.at[to], rs_in.at[d], rs_s.at[d], rs_r.at[d], 2 * to + c, l)

    @pl.loop(1, CHIPS)
    def _(d):
        to = (j + d) % CHIPS
        c_copy(to).wait_recv()
        rs_out[to] = (c_own[to] + c_in[to].astype(F32)).astype(BF16)
        rs_copy(d).start()

    c_copy(j).wait_recv()
    c_own[j] = c_own[j] + c_in[j].astype(F32)

    gather_finish(1, f_all)
    l_bu.wait()

    @pl.loop(0, 4)
    def _(i):
        at = pl.ds(pl.multiple_of(i * ROWS, ROWS), ROWS)
        low = jnp.dot(u_v[at, :], f_all[...], preferred_element_type=F32)
        bu_v[at, :] = (bu_v[at, :].astype(F32) - low).astype(BF16)

    o_u = pltpu.make_async_copy(bu_v, out_u, loc.at[22])
    o_u.start()

    @pl.loop(1, CHIPS)
    def _(d):
        rs_copy(d).wait_recv()
        c_own[j] = c_own[j] + rs_in[d].astype(F32)

    mine = pl.ds(pl.multiple_of(f * ROWS, ROWS), ROWS)
    red_all[mine, :] = (f_all[mine, :].astype(F32) - c_own[j]).astype(BF16)
    gather_start(2, red_all)

    l_pc.wait()

    @pl.loop(1, 16)
    def _(d):
        p_recv(d).wait_recv()

    @pl.loop(0, 16)
    def _(i):
        at = pl.ds(pl.multiple_of(i * ROWS, ROWS), ROWS)
        pt[:, at] = pc[i].T

    gather_forward(2, red_all)

    @pl.loop(0, 8)
    def _(i):
        w_copy(i).wait_recv()
        w_core(i).start()

    gather_finish(2, red_all)
    sol = jnp.dot(pt[...], red_all[...], preferred_element_type=F32).astype(BF16)
    s_all[z] = sol
    o_s = pltpu.make_async_copy(s_all.at[z], out_s, loc.at[23])
    o_s.start()

    def piece(i, q):
        n = ROWS // PIECES
        return s_all.at[i, pl.ds(pl.multiple_of(q * n, n), n)]

    def up(t, q):
        it = piece((z + 16 - t) % 16, q)
        return rdma(it, it, zs.at[0, t, q], zr.at[0, t, q], f, (l + 2) % 32)

    def up_recv(t, q):
        it = piece((z + 15 - t) % 16, q)
        return rdma(it, it, zs.at[0, t, q], zr.at[0, t, q], sib, l)

    def down(t, q):
        it = piece((z + t) % 16, q)
        return rdma(it, it, zs.at[1, t, q], zr.at[1, t, q], f, (l + 30) % 32)

    def down_recv(t, q):
        it = piece((z + t + 1) % 16, q)
        return rdma(it, it, zs.at[1, t, q], zr.at[1, t, q], sib, l)

    def product(i):
        return lax.dot_general(w2[i], s_all[i], (((1,), (1,)), ((), ())), preferred_element_type=F32)

    for q in range(PIECES):
        up(0, q).start()
        down(0, q).start()

    @pl.loop(0, 16)
    def _(i):
        l_w(i).wait()

    @pl.loop(0, 8)
    def _(i):
        w_core_recv(i).wait_recv()

    r_acc[...] = product(z)

    @pl.loop(1, 7)
    def _(t):
        for q in range(PIECES):
            up_recv(t - 1, q).wait_recv()
            up(t, q).start()
            down_recv(t - 1, q).wait_recv()
            down(t, q).start()
        r_acc[...] += product((z + 16 - t) % 16) + product((z + t) % 16)

    for q in range(PIECES):
        up_recv(6, q).wait_recv()
        up(7, q).start()
    r_acc[...] += product((z + 9) % 16)
    for q in range(PIECES):
        down_recv(6, q).wait_recv()
    r_acc[...] += product((z + 7) % 16)
    for q in range(PIECES):
        up_recv(7, q).wait_recv()
    r_acc[...] += product((z + 8) % 16)

    swap = rdma(r_acc.at[pl.ds(96, 96)], r_in, r_s.at[0], r_s.at[1], f, 2 * z + 1 - s)
    swap.start()

    for k, buf in enumerate((bp_all, f_all, red_all)):
        gather_sent(k, buf)

    @pl.loop(1, 32)
    def _(d):
        x_copy(d).wait_send()

    @pl.loop(1, 16)
    def _(d):
        p_copy(d).wait_send()

    @pl.loop(0, 8)
    def _(i):
        w_copy(i).wait_send()
        w_core(i).wait_send()
        c_copy(i).wait_send()

    @pl.loop(1, CHIPS)
    def _(d):
        rs_copy(d).wait_send()

    @pl.loop(0, 7)
    def _(t):
        for q in range(PIECES):
            up(t, q).wait_send()
            down(t, q).wait_send()

    for q in range(PIECES):
        up(7, q).wait_send()
    o_u.wait()
    o_s.wait()
    swap.wait()
    r_in[...] = r_acc[pl.ds(0, 96), :] + r_in[...]
    o_r = pltpu.make_async_copy(r_in, out_r, loc.at[24])
    o_r.start()
    o_r.wait()


def local(bp, bu, pinv, uf, xs, ws):
    dma = pltpu.SemaphoreType.DMA
    vm = pltpu.VMEM
    hbm = pl.BlockSpec(memory_space=pl.ANY)
    return pl.pallas_call(
        kernel,
        name="solves",
        out_shape=(
            jax.ShapeDtypeStruct((512, COLS), BF16),
            jax.ShapeDtypeStruct((ROWS, COLS), BF16),
            jax.ShapeDtypeStruct((96, ROWS), F32),
        ),
        in_specs=[hbm] * 6,
        out_specs=(hbm,) * 3,
        scratch_shapes=[
            vm((2048, COLS), BF16), vm((2048, COLS), BF16), vm((2048, COLS), BF16),
            vm((ROWS, 2048), BF16), vm((16, ROWS, ROWS), BF16), vm((ROWS, 2048), BF16),
            vm((512, 2048), BF16), vm((2048, 512), BF16), vm((512, COLS), BF16), vm((512, COLS), BF16),
            vm((16, 192, COLS), BF16), vm((16, ROWS, COLS), BF16),
            vm((CHIPS, ROWS, COLS), BF16), vm((CHIPS, ROWS, COLS), BF16), vm((CHIPS, ROWS, COLS), F32),
            vm((CHIPS, ROWS, COLS), BF16), vm((CHIPS, ROWS, COLS), BF16),
            vm((192, ROWS), F32), vm((96, ROWS), F32),
            dma((25,)), dma((32,)), dma((32,)), dma((3, 8)), dma((3, 8)), dma((3, 8)), dma((3, 8)),
            dma((16,)), dma((16,)), dma((16,)), dma((16,)), dma((8,)), dma((8,)), dma((8,)), dma((8,)),
            dma((2, 8, PIECES)), dma((2, 8, PIECES)), dma((2,)),
        ],
        compiler_params=pltpu.CompilerParams(
            collective_id=0, has_side_effects=True, vmem_limit_bytes=56 << 20
        ),
    )(bp, bu, pinv, uf, xs, ws)


def solution(mesh):
    in_specs = (
        P("factor", "load"),
        P("factor", "load"),
        P("factor", None),
        P("factor", None),
        P(("factor", "load"), None),
        P("load", None),
    )
    out_specs = (P("factor", "load"), P("factor", "load"), P("load", "factor"))
    return jax.shard_map(local, mesh=mesh, in_specs=in_specs, out_specs=out_specs, check_vma=False)
```

```python
import functools

import jax
import jax.numpy as jnp
from jax import lax
from jax.experimental import pallas as pl
from jax.experimental.pallas import tpu as pltpu
from jax.sharding import PartitionSpec as P

MESH = pl.DeviceIdType.MESH
BF16 = jnp.bfloat16
F32 = jnp.float32
CHIPS = 8
ROWS = 128
COLS = 256


def kernel(
    bp, bu, pinv, uf, xs, ws, out_u, out_s, out_r,
    bp_all, f_all, red_all, p_v, pc, pt, u_v, ut, x_r, bu_v, w2, s_all,
    c_out, c_in, c_own, rs_out, rs_in, r_acc, r_in,
    loc, x_s, x_rv, ag_s, ag_r, sib_s, sib_r, p_s, p_r, w_s, w_r, c_s, c_r, rs_s, rs_r, fs, fr, ns, nr, r_s,
):
    f = lax.axis_index("factor")
    l = lax.axis_index("load")
    j, c = f // 2, f % 2
    h, y = j // 4, j % 4
    z, s = l // 2, l % 2
    sib = 2 * j + 1 - c

    pending = {}

    def settle(name):
        pending.pop(name)()

    def later(name, copy, lo, hi, how):
        def run():
            @pl.loop(lo, hi)
            def _(i):
                getattr(copy(i), how)()

        pending[name] = run

    def rdma(src, dst, ss, rs, df, dl):
        return pltpu.make_async_remote_copy(
            src_ref=src, dst_ref=dst, send_sem=ss, recv_sem=rs,
            device_id={"factor": df, "load": dl}, device_id_type=MESH,
        )

    def rows(ref, i, n=ROWS):
        return ref.at[pl.ds(pl.multiple_of(i * n, n), n)]

    def cols(ref, i, n):
        return ref.at[:, pl.ds(pl.multiple_of(i * n, n), n)]

    l_u = pltpu.make_async_copy(uf, u_v, loc.at[0])
    l_p = pltpu.make_async_copy(pinv, p_v, loc.at[1])
    l_b = pltpu.make_async_copy(bp, rows(bp_all, f), loc.at[2])
    l_x = pltpu.make_async_copy(cols(xs, l, COLS), rows(x_r, l, 16), loc.at[3])
    l_bu = pltpu.make_async_copy(bu, bu_v, loc.at[4])
    l_pc = pltpu.make_async_copy(cols(pinv, f, ROWS), pc.at[f], loc.at[5])
    for at, cp in enumerate((l_b, l_p, l_x, l_u, l_bu, l_pc)):
        cp.start()
        pending["l%d" % at] = cp.wait

    def l_w(i):
        return pltpu.make_async_copy(cols(ws, 2 * i + s, COLS), w2.at[i, pl.ds(0, 96)], loc.at[6 + i])

    @pl.loop(0, 16)
    def _(i):
        l_w(i).start()

    later("w own", l_w, 0, 16, "wait")

    barrier = pltpu.get_barrier_semaphore()

    def hello(df, dl):
        pl.semaphore_signal(barrier, inc=1, device_id={"factor": df, "load": dl}, device_id_type=MESH)

    @pl.loop(1, 32)
    def _(d):
        hello(f, (l + d) % 32)

    @pl.loop(1, 8)
    def _(d):
        hello(h * 8 + (f + d) % 8, l)

    @pl.loop(0, 8)
    def _(d):
        hello((1 - h) * 8 + d, 2 * z + 1 - s)

    @pl.loop(0, 4)
    def _(d):
        hello((1 - h) * 8 + 2 * d + c, l)

    pl.semaphore_wait(barrier, 31 + 7 + 8 + 4)

    def chip_copy(k, buf, d):
        own = rows(buf, f)
        return rdma(own, own, ag_s.at[k, d], ag_r.at[k, d], 2 * ((j + d) % CHIPS) + c, l)

    def chip_recv(k, buf, d):
        got = rows(buf, 2 * ((j + CHIPS - d) % CHIPS) + c)
        return rdma(got, got, ag_s.at[k, d], ag_r.at[k, d], sib, l)

    def core_copy(k, buf, d):
        got = rows(buf, 2 * ((j + CHIPS - d) % CHIPS) + c)
        return rdma(got, got, sib_s.at[k, d], sib_r.at[k, d], sib, l)

    def gather_start(k, buf):
        @pl.loop(1, CHIPS)
        def _(d):
            chip_copy(k, buf, d).start()

        core_copy(k, buf, 0).start()
        later(("chips sent", k), lambda d: chip_copy(k, buf, d), 1, CHIPS, "wait_send")
        later(("cores sent", k), lambda d: core_copy(k, buf, d), 0, CHIPS, "wait_send")
        later(("cores", k), lambda d: core_copy(k, buf, d), 0, CHIPS, "wait_recv")

    def gather_forward(k, buf):
        @pl.loop(1, CHIPS)
        def _(d):
            chip_recv(k, buf, d).wait_recv()
            core_copy(k, buf, d).start()

    def x_copy(d):
        to = (l + d) % 32
        return rdma(cols(xs, to, COLS), rows(x_r, l, 16), x_s.at[d], x_rv.at[d], f, to)

    def x_recv(d):
        got = rows(x_r, (l + 32 - d) % 32, 16)
        return rdma(got, got, x_s.at[d], x_rv.at[d], f, l)

    settle("l0")
    gather_start(0, bp_all)

    @pl.loop(1, 32)
    def _(d):
        x_copy(d).start()

    later("x sent", x_copy, 1, 32, "wait_send")
    later("x", x_recv, 1, 32, "wait_recv")

    def p_copy(d):
        to = (f + d) % 16
        same = 1 - (to // 8 + h) % 2
        dl = 2 * z + same * s + (1 - same) * (1 - s)
        return rdma(cols(p_v, to, ROWS), pc.at[f], p_s.at[d], p_r.at[d], to, dl)

    def p_recv(d):
        got = pc.at[(f + 16 - d) % 16]
        return rdma(got, got, p_s.at[d], p_r.at[d], sib, l)

    def w_copy(i):
        zz = 8 * c + i
        return rdma(
            cols(ws, 2 * zz + 1 - s, COLS), w2.at[zz, pl.ds(96, 96)], w_s.at[i], w_r.at[i], f, 2 * z + 1 - s
        )

    def w_core(i):
        got = w2.at[8 * c + i, pl.ds(96, 96)]
        return rdma(got, got, w_s.at[8 + i], w_r.at[8 + i], sib, l)

    def w_core_recv(i):
        got = w2.at[8 * (1 - c) + i, pl.ds(96, 96)]
        return rdma(got, got, w_s.at[8 + i], w_r.at[8 + i], sib, l)

    settle("l1")

    @pl.loop(1, 16)
    def _(d):
        p_copy(d).start()

    later("p sent", p_copy, 1, 16, "wait_send")
    later("p", p_recv, 1, 16, "wait_recv")

    @pl.loop(0, 8)
    def _(i):
        w_copy(i).start()

    later("w sent", w_copy, 0, 8, "wait_send")
    later("w", w_copy, 0, 8, "wait_recv")

    gather_forward(0, bp_all)

    settle(("cores", 0))
    fwd = jnp.dot(p_v[...], bp_all[...], preferred_element_type=F32).astype(BF16)
    f_all[pl.ds(pl.multiple_of(f * ROWS, ROWS), ROWS), :] = fwd

    settle("l3")

    @pl.loop(0, 16)
    def _(i):
        at = pl.ds(pl.multiple_of(i * ROWS, ROWS), ROWS)
        ut[at, :] = u_v[:, at].T

    settle("l2")

    settle("x")

    def c_copy(i):
        return rdma(c_out.at[i], c_in.at[i], c_s.at[i], c_r.at[i], sib, l)

    def partial(i, core):
        at = pl.ds(pl.multiple_of((2 * i + core) * ROWS, ROWS), ROWS)
        return jnp.dot(ut[at, :], x_r[...], preferred_element_type=F32)

    @pl.loop(0, CHIPS)
    def _(i):
        c_out[i] = partial(i, 1 - c).astype(BF16)
        c_copy(i).start()

    later("c sent", c_copy, 0, CHIPS, "wait_send")

    @pl.loop(0, CHIPS)
    def _(i):
        c_own[i] = partial(i, c)

    def rs_copy(d):
        to = (j + d) % CHIPS
        return rdma(rs_out.at[to], rs_in.at[d], rs_s.at[d], rs_r.at[d], 2 * to + c, l)

    @pl.loop(1, CHIPS)
    def _(d):
        to = (j + d) % CHIPS
        c_copy(to).wait_recv()
        rs_out[to] = (c_own[to] + c_in[to].astype(F32)).astype(BF16)
        rs_copy(d).start()

    later("rs sent", rs_copy, 1, CHIPS, "wait_send")
    c_copy(j).wait_recv()
    c_own[j] = c_own[j] + c_in[j].astype(F32)

    @pl.loop(1, CHIPS)
    def _(d):
        rs_copy(d).wait_recv()
        c_own[j] = c_own[j] + rs_in[d].astype(F32)

    mine = pl.ds(pl.multiple_of(f * ROWS, ROWS), ROWS)
    red_all[mine, :] = (f_all[mine, :].astype(F32) - c_own[j]).astype(BF16)
    gather_start(2, red_all)

    settle("l5")

    settle("p")

    @pl.loop(0, 16)
    def _(i):
        at = pl.ds(pl.multiple_of(i * ROWS, ROWS), ROWS)
        pt[:, at] = pc[i].T

    gather_forward(2, red_all)

    settle("w")

    @pl.loop(0, 8)
    def _(i):
        w_core(i).start()

    later("w core sent", w_core, 0, 8, "wait_send")
    later("w core", w_core_recv, 0, 8, "wait_recv")

    settle(("cores", 2))
    sol = jnp.dot(pt[...], red_all[...], preferred_element_type=F32).astype(BF16)
    s_all[z] = sol
    o_s = pltpu.make_async_copy(s_all.at[z], out_s, loc.at[23])
    o_s.start()

    HALF = ROWS // 2
    legs = ((0, 1), (1, -1), (1, 1), (0, -1))

    def half(i, q):
        return s_all.at[i, pl.ds(q * HALF, HALF)]

    def last(q, way):
        return 4 if way == (1 - 2 * q) else 3

    def far(q, way, k):
        it = half((z + 32 - way * 2 * k) % 16, q)
        at = (q, (1 - way) // 2, k)
        return rdma(it, it, fs.at[at], fr.at[at], f, (l + 64 + 4 * way) % 32)

    def far_recv(q, way, k):
        it = half((z + 32 - way * (2 * k + 2)) % 16, q)
        at = (q, (1 - way) // 2, k)
        return rdma(it, it, fs.at[at], fr.at[at], sib, l)

    def near(q, way, k):
        it = half((z + 32 - way * 2 * k) % 16, q)
        at = (q, (1 - way) // 2, k)
        return rdma(it, it, ns.at[at], nr.at[at], f, (l + 64 + 2 * way) % 32)

    def near_recv(q, way, k):
        it = half((z + 32 - way * (2 * k + 1)) % 16, q)
        at = (q, (1 - way) // 2, k)
        return rdma(it, it, ns.at[at], nr.at[at], sib, l)

    def product(i):
        return lax.dot_general(w2[i % 16], s_all[i % 16], (((1,), (1,)), ((), ())), preferred_element_type=F32)

    for q, way in legs:
        far(q, way, 0).start()
    for q, way in legs:
        near(q, way, 0).start()
        later(("far sent", q, way), lambda k, q=q, way=way: far(q, way, k), 0, last(q, way), "wait_send")
        later(("near sent", q, way), lambda k, q=q, way=way: near(q, way, k), 0, 4, "wait_send")
    gather_start(1, f_all)
    settle("w own")
    settle("w core")
    r_acc[...] = product(z)
    for k in range(1, 4):
        for q, way in legs:
            far_recv(q, way, k - 1).wait_recv()
            if k < last(q, way):
                far(q, way, k).start()
        for q, way in legs:
            near(q, way, k).start()
        if k == 3:
            gather_forward(1, f_all)
        r_acc[...] += product(z + 2 * k) + product(z + 16 - 2 * k)
        for q, way in legs:
            near_recv(q, way, k - 1).wait_recv()
        r_acc[...] += product(z + 2 * k - 1) + product(z + 17 - 2 * k)

    settle(("cores", 1))
    settle("l4")

    @pl.loop(0, 4)
    def _(i):
        at = pl.ds(pl.multiple_of(i * ROWS, ROWS), ROWS)
        low = jnp.dot(u_v[at, :], f_all[...], preferred_element_type=F32)
        bu_v[at, :] = (bu_v[at, :].astype(F32) - low).astype(BF16)

    o_u = pltpu.make_async_copy(bu_v, out_u, loc.at[22])
    o_u.start()

    for q, way in legs:
        near_recv(q, way, 3).wait_recv()
    r_acc[...] += product(z + 7) + product(z + 9)
    for q, way in legs[:2]:
        far_recv(q, way, 3).wait_recv()
    r_acc[...] += product(z + 8)

    swap = rdma(r_acc.at[pl.ds(96, 96)], r_in, r_s.at[0], r_s.at[1], f, 2 * z + 1 - s)
    swap.start()

    for name in list(pending):
        settle(name)
    o_u.wait()
    o_s.wait()
    swap.wait()
    r_in[...] = r_acc[pl.ds(0, 96), :] + r_in[...]
    o_r = pltpu.make_async_copy(r_in, out_r, loc.at[24])
    o_r.start()
    o_r.wait()


def leave(u, s, r, out_u, out_s, out_r):
    out_u[...] = u[...]
    out_s[...] = s[...]
    out_r[...] = r[...]


def local(bp, bu, pinv, uf, xs, ws):
    dma = pltpu.SemaphoreType.DMA
    vm = pltpu.VMEM
    hbm = pl.BlockSpec(memory_space=pl.ANY)
    outs = (
        jax.ShapeDtypeStruct((512, COLS), BF16),
        jax.ShapeDtypeStruct((ROWS, COLS), BF16),
        jax.ShapeDtypeStruct((96, ROWS), F32),
    )
    results = pl.pallas_call(
        kernel,
        name="solves",
        out_shape=outs,
        in_specs=[hbm] * 6,
        out_specs=(hbm,) * 3,
        scratch_shapes=[
            vm((2048, COLS), BF16), vm((2048, COLS), BF16), vm((2048, COLS), BF16),
            vm((ROWS, 2048), BF16), vm((16, ROWS, ROWS), BF16), vm((ROWS, 2048), BF16),
            vm((512, 2048), BF16), vm((2048, 512), BF16), vm((512, COLS), BF16), vm((512, COLS), BF16),
            vm((16, 192, COLS), BF16), vm((16, ROWS, COLS), BF16),
            vm((CHIPS, ROWS, COLS), BF16), vm((CHIPS, ROWS, COLS), BF16), vm((CHIPS, ROWS, COLS), F32),
            vm((CHIPS, ROWS, COLS), BF16), vm((CHIPS, ROWS, COLS), BF16),
            vm((192, ROWS), F32), vm((96, ROWS), F32),
            dma((25,)), dma((32,)), dma((32,)), dma((3, 8)), dma((3, 8)), dma((3, 8)), dma((3, 8)),
            dma((16,)), dma((16,)), dma((16,)), dma((16,)), dma((8,)), dma((8,)), dma((8,)), dma((8,)),
            dma((2, 2, 4)), dma((2, 2, 4)), dma((2, 2, 4)), dma((2, 2, 4)), dma((2,)),
        ],
        compiler_params=pltpu.CompilerParams(
            collective_id=0, has_side_effects=True, vmem_limit_bytes=56 << 20
        ),
    )(bp, bu, pinv, uf, xs, ws)
    return pl.pallas_call(
        leave,
        name="leave",
        out_shape=outs,
        in_specs=[pl.BlockSpec(memory_space=vm)] * 3,
        out_specs=(pl.BlockSpec(memory_space=vm),) * 3,
    )(*results)


def solution(mesh):
    in_specs = (
        P("factor", "load"),
        P("factor", "load"),
        P("factor", None),
        P("factor", None),
        P(("factor", "load"), None),
        P("load", None),
    )
    out_specs = (P("factor", "load"), P("factor", "load"), P("load", "factor"))
    return jax.shard_map(local, mesh=mesh, in_specs=in_specs, out_specs=out_specs, check_vma=False)
```

```python
import functools

import jax
import jax.numpy as jnp
from jax import lax
from jax.experimental import pallas as pl
from jax.experimental.pallas import tpu as pltpu
from jax.sharding import PartitionSpec as P

MESH = pl.DeviceIdType.MESH
BF16 = jnp.bfloat16
F32 = jnp.float32
CHIPS = 8
ROWS = 128
COLS = 256


def kernel(
    bp, bu, pinv, uf, xs, ws, out_u, out_s, out_r,
    bp_all, f_all, red_all, p_v, pc, pt, u_v, ut, x_r, bu_v, w2, z_all, s_v, t_all,
    c_out, c_in, c_own, rs_out, rs_in, r_acc, r_in, r_sum,
    loc, x_s, x_rv, ag_s, ag_r, sib_s, sib_r, p_s, p_r, w_s, w_r, c_s, c_r, rs_s, rs_r, fs, fr, ns, nr, r_s,
):
    f = lax.axis_index("factor")
    l = lax.axis_index("load")
    j, c = f // 2, f % 2
    h, y = j // 4, j % 4
    z, s = l // 2, l % 2
    sib = 2 * j + 1 - c

    pending = {}

    def settle(name):
        pending.pop(name)()

    def later(name, copy, lo, hi, how):
        def run():
            @pl.loop(lo, hi)
            def _(i):
                getattr(copy(i), how)()

        pending[name] = run

    def rdma(src, dst, ss, rs, df, dl):
        return pltpu.make_async_remote_copy(
            src_ref=src, dst_ref=dst, send_sem=ss, recv_sem=rs,
            device_id={"factor": df, "load": dl}, device_id_type=MESH,
        )

    def rows(ref, i, n=ROWS):
        return ref.at[pl.ds(pl.multiple_of(i * n, n), n)]

    def cols(ref, i, n):
        return ref.at[:, pl.ds(pl.multiple_of(i * n, n), n)]

    l_u = pltpu.make_async_copy(uf, u_v, loc.at[0])
    l_p = pltpu.make_async_copy(pinv, p_v, loc.at[1])
    l_b = pltpu.make_async_copy(bp, rows(bp_all, f), loc.at[2])
    l_x = pltpu.make_async_copy(cols(xs, l, COLS), rows(x_r, l, 16), loc.at[3])
    l_bu = pltpu.make_async_copy(bu, bu_v, loc.at[4])
    l_pc = pltpu.make_async_copy(cols(pinv, f, ROWS), pc.at[f], loc.at[5])
    for at, cp in enumerate((l_b, l_p, l_x, l_u, l_bu, l_pc)):
        cp.start()
        pending["l%d" % at] = cp.wait

    def l_w(i):
        return pltpu.make_async_copy(cols(ws, 2 * i + s, COLS), w2.at[i, pl.ds(0, 96)], loc.at[6 + i])

    @pl.loop(0, 16)
    def _(i):
        l_w(i).start()

    later("w own", l_w, 0, 16, "wait")

    barrier = pltpu.get_barrier_semaphore()

    def hello(df, dl):
        pl.semaphore_signal(barrier, inc=1, device_id={"factor": df, "load": dl}, device_id_type=MESH)

    @pl.loop(1, 32)
    def _(d):
        hello(f, (l + d) % 32)

    @pl.loop(1, 8)
    def _(d):
        hello(h * 8 + (f + d) % 8, l)

    @pl.loop(0, 8)
    def _(d):
        hello((1 - h) * 8 + d, 2 * z + 1 - s)

    @pl.loop(0, 4)
    def _(d):
        hello((1 - h) * 8 + 2 * d + c, l)

    pl.semaphore_wait(barrier, 31 + 7 + 8 + 4)

    size = (ROWS, ROWS, ROWS, 96)

    def chip_copy(k, buf, d):
        own = rows(buf, f, size[k])
        return rdma(own, own, ag_s.at[k, d], ag_r.at[k, d], 2 * ((j + d) % CHIPS) + c, l)

    def chip_recv(k, buf, d):
        got = rows(buf, 2 * ((j + CHIPS - d) % CHIPS) + c, size[k])
        return rdma(got, got, ag_s.at[k, d], ag_r.at[k, d], sib, l)

    def core_copy(k, buf, d):
        got = rows(buf, 2 * ((j + CHIPS - d) % CHIPS) + c, size[k])
        return rdma(got, got, sib_s.at[k, d], sib_r.at[k, d], sib, l)

    def gather_start(k, buf):
        @pl.loop(1, CHIPS)
        def _(d):
            chip_copy(k, buf, d).start()

        core_copy(k, buf, 0).start()
        later(("chips sent", k), lambda d: chip_copy(k, buf, d), 1, CHIPS, "wait_send")
        later(("cores sent", k), lambda d: core_copy(k, buf, d), 0, CHIPS, "wait_send")
        later(("cores", k), lambda d: core_copy(k, buf, d), 0, CHIPS, "wait_recv")

    def gather_forward(k, buf):
        @pl.loop(1, CHIPS)
        def _(d):
            chip_recv(k, buf, d).wait_recv()
            core_copy(k, buf, d).start()

    def x_copy(d):
        to = (l + d) % 32
        return rdma(cols(xs, to, COLS), rows(x_r, l, 16), x_s.at[d], x_rv.at[d], f, to)

    def x_recv(d):
        got = rows(x_r, (l + 32 - d) % 32, 16)
        return rdma(got, got, x_s.at[d], x_rv.at[d], f, l)

    settle("l0")
    gather_start(0, bp_all)

    @pl.loop(1, 32)
    def _(d):
        x_copy(d).start()

    later("x sent", x_copy, 1, 32, "wait_send")
    later("x", x_recv, 1, 32, "wait_recv")

    def p_copy(d):
        to = (f + d) % 16
        same = 1 - (to // 8 + h) % 2
        dl = 2 * z + same * s + (1 - same) * (1 - s)
        return rdma(cols(p_v, to, ROWS), pc.at[f], p_s.at[d], p_r.at[d], to, dl)

    def p_recv(d):
        got = pc.at[(f + 16 - d) % 16]
        return rdma(got, got, p_s.at[d], p_r.at[d], sib, l)

    def w_copy(i):
        zz = 8 * c + i
        return rdma(
            cols(ws, 2 * zz + 1 - s, COLS), w2.at[zz, pl.ds(96, 96)], w_s.at[i], w_r.at[i], f, 2 * z + 1 - s
        )

    def w_core(i):
        got = w2.at[8 * c + i, pl.ds(96, 96)]
        return rdma(got, got, w_s.at[8 + i], w_r.at[8 + i], sib, l)

    def w_core_recv(i):
        got = w2.at[8 * (1 - c) + i, pl.ds(96, 96)]
        return rdma(got, got, w_s.at[8 + i], w_r.at[8 + i], sib, l)

    settle("l1")

    @pl.loop(1, 16)
    def _(d):
        p_copy(d).start()

    later("p sent", p_copy, 1, 16, "wait_send")
    later("p", p_recv, 1, 16, "wait_recv")

    @pl.loop(0, 8)
    def _(i):
        w_copy(i).start()

    later("w sent", w_copy, 0, 8, "wait_send")
    later("w", w_copy, 0, 8, "wait_recv")

    gather_forward(0, bp_all)

    settle(("cores", 0))
    fwd = jnp.dot(p_v[...], bp_all[...], preferred_element_type=F32).astype(BF16)
    f_all[pl.ds(pl.multiple_of(f * ROWS, ROWS), ROWS), :] = fwd

    settle("l3")

    @pl.loop(0, 16)
    def _(i):
        at = pl.ds(pl.multiple_of(i * ROWS, ROWS), ROWS)
        ut[at, :] = u_v[:, at].T

    settle("l2")

    settle("x")

    def c_copy(i):
        return rdma(c_out.at[i], c_in.at[i], c_s.at[i], c_r.at[i], sib, l)

    def partial(i, core):
        at = pl.ds(pl.multiple_of((2 * i + core) * ROWS, ROWS), ROWS)
        return jnp.dot(ut[at, :], x_r[...], preferred_element_type=F32)

    @pl.loop(0, CHIPS)
    def _(i):
        c_out[i] = partial(i, 1 - c).astype(BF16)
        c_copy(i).start()

    later("c sent", c_copy, 0, CHIPS, "wait_send")

    @pl.loop(0, CHIPS)
    def _(i):
        c_own[i] = partial(i, c)

    def rs_copy(d):
        to = (j + d) % CHIPS
        return rdma(rs_out.at[to], rs_in.at[d], rs_s.at[d], rs_r.at[d], 2 * to + c, l)

    @pl.loop(1, CHIPS)
    def _(d):
        to = (j + d) % CHIPS
        c_copy(to).wait_recv()
        rs_out[to] = (c_own[to] + c_in[to].astype(F32)).astype(BF16)
        rs_copy(d).start()

    later("rs sent", rs_copy, 1, CHIPS, "wait_send")
    c_copy(j).wait_recv()
    c_own[j] = c_own[j] + c_in[j].astype(F32)

    settle("l5")

    settle("p")

    @pl.loop(0, 16)
    def _(i):
        at = pl.ds(pl.multiple_of(i * ROWS, ROWS), ROWS)
        pt[:, at] = pc[i].T

    settle("w")

    @pl.loop(0, 8)
    def _(i):
        w_core(i).start()

    later("w core sent", w_core, 0, 8, "wait_send")
    later("w core", w_core_recv, 0, 8, "wait_recv")

    @pl.loop(1, CHIPS)
    def _(d):
        rs_copy(d).wait_recv()
        c_own[j] = c_own[j] + rs_in[d].astype(F32)

    mine = pl.ds(pl.multiple_of(f * ROWS, ROWS), ROWS)
    red = (f_all[mine, :].astype(F32) - c_own[j]).astype(BF16)
    z_all[z] = red
    red_all[mine, :] = red

    HALF = ROWS // 2
    legs = ((0, 1), (1, -1), (1, 1), (0, -1))

    def half(i, q):
        return z_all.at[i, pl.ds(q * HALF, HALF)]

    def last(q, way):
        return 4 if way == (1 - 2 * q) else 3

    def far(q, way, k):
        it = half((z + 32 - way * 2 * k) % 16, q)
        at = (q, (1 - way) // 2, k)
        return rdma(it, it, fs.at[at], fr.at[at], f, (l + 64 + 4 * way) % 32)

    def far_recv(q, way, k):
        it = half((z + 32 - way * (2 * k + 2)) % 16, q)
        at = (q, (1 - way) // 2, k)
        return rdma(it, it, fs.at[at], fr.at[at], sib, l)

    def near(q, way, k):
        it = half((z + 32 - way * 2 * k) % 16, q)
        at = (q, (1 - way) // 2, k)
        return rdma(it, it, ns.at[at], nr.at[at], f, (l + 64 + 2 * way) % 32)

    def near_recv(q, way, k):
        it = half((z + 32 - way * (2 * k + 1)) % 16, q)
        at = (q, (1 - way) // 2, k)
        return rdma(it, it, ns.at[at], nr.at[at], sib, l)

    def product(i):
        return lax.dot_general(w2[i % 16], z_all[i % 16], (((1,), (1,)), ((), ())), preferred_element_type=F32)

    for q, way in legs:
        far(q, way, 0).start()
    for q, way in legs:
        near(q, way, 0).start()
        later(("far sent", q, way), lambda k, q=q, way=way: far(q, way, k), 0, last(q, way), "wait_send")
        later(("near sent", q, way), lambda k, q=q, way=way: near(q, way, k), 0, 4, "wait_send")
    gather_start(2, red_all)
    settle("w own")
    settle("w core")
    r_acc[...] = product(z)
    for k in range(1, 4):
        for q, way in legs:
            far_recv(q, way, k - 1).wait_recv()
            if k < last(q, way):
                far(q, way, k).start()
        for q, way in legs:
            near(q, way, k).start()
        if k == 2:
            gather_start(1, f_all)
        if k == 3:
            gather_forward(2, red_all)
        r_acc[...] += product(z + 2 * k) + product(z + 16 - 2 * k)
        for q, way in legs:
            near_recv(q, way, k - 1).wait_recv()
        r_acc[...] += product(z + 2 * k - 1) + product(z + 17 - 2 * k)

    for q, way in legs:
        near_recv(q, way, 3).wait_recv()
    r_acc[...] += product(z + 7) + product(z + 9)
    for q, way in legs[:2]:
        far_recv(q, way, 3).wait_recv()
    r_acc[...] += product(z + 8)

    swap = rdma(r_acc.at[pl.ds(96, 96)], r_in, r_s.at[0], r_s.at[1], f, 2 * z + 1 - s)
    swap.start()
    gather_forward(1, f_all)
    swap.wait_recv()
    t_all[pl.ds(pl.multiple_of(f * 96, 96), 96), :] = (r_acc[pl.ds(0, 96), :] + r_in[...]).astype(BF16)
    gather_start(3, t_all)

    settle(("cores", 2))
    s_v[...] = jnp.dot(pt[...], red_all[...], preferred_element_type=F32).astype(BF16)
    o_s = pltpu.make_async_copy(s_v, out_s, loc.at[23])
    o_s.start()
    settle(("cores", 1))
    settle("l4")

    @pl.loop(0, 4)
    def _(i):
        at = pl.ds(pl.multiple_of(i * ROWS, ROWS), ROWS)
        low = jnp.dot(u_v[at, :], f_all[...], preferred_element_type=F32)
        bu_v[at, :] = (bu_v[at, :].astype(F32) - low).astype(BF16)

    o_u = pltpu.make_async_copy(bu_v, out_u, loc.at[22])
    o_u.start()

    gather_forward(3, t_all)
    settle(("cores", 3))
    r_sum[...] = jnp.zeros((96, ROWS), F32)

    @pl.loop(0, 16)
    def _(i):
        r_sum[...] += jnp.dot(
            t_all[pl.ds(pl.multiple_of(i * 96, 96), 96), :], pc[i], preferred_element_type=F32
        )

    o_r = pltpu.make_async_copy(r_sum, out_r, loc.at[24])
    o_r.start()

    for name in list(pending):
        settle(name)
    o_u.wait()
    o_s.wait()
    swap.wait_send()
    o_r.wait()


def leave(u, s, r, out_u, out_s, out_r):
    out_u[...] = u[...]
    out_s[...] = s[...]
    out_r[...] = r[...]


def local(bp, bu, pinv, uf, xs, ws):
    dma = pltpu.SemaphoreType.DMA
    vm = pltpu.VMEM
    hbm = pl.BlockSpec(memory_space=pl.ANY)
    outs = (
        jax.ShapeDtypeStruct((512, COLS), BF16),
        jax.ShapeDtypeStruct((ROWS, COLS), BF16),
        jax.ShapeDtypeStruct((96, ROWS), F32),
    )
    results = pl.pallas_call(
        kernel,
        name="solves",
        out_shape=outs,
        in_specs=[hbm] * 6,
        out_specs=(hbm,) * 3,
        scratch_shapes=[
            vm((2048, COLS), BF16), vm((2048, COLS), BF16), vm((2048, COLS), BF16),
            vm((ROWS, 2048), BF16), vm((16, ROWS, ROWS), BF16), vm((ROWS, 2048), BF16),
            vm((512, 2048), BF16), vm((2048, 512), BF16), vm((512, COLS), BF16), vm((512, COLS), BF16),
            vm((16, 192, COLS), BF16), vm((16, ROWS, COLS), BF16), vm((ROWS, COLS), BF16), vm((16 * 96, ROWS), BF16),
            vm((CHIPS, ROWS, COLS), BF16), vm((CHIPS, ROWS, COLS), BF16), vm((CHIPS, ROWS, COLS), F32),
            vm((CHIPS, ROWS, COLS), BF16), vm((CHIPS, ROWS, COLS), BF16),
            vm((192, ROWS), F32), vm((96, ROWS), F32), vm((96, ROWS), F32),
            dma((25,)), dma((32,)), dma((32,)), dma((4, 8)), dma((4, 8)), dma((4, 8)), dma((4, 8)),
            dma((16,)), dma((16,)), dma((16,)), dma((16,)), dma((8,)), dma((8,)), dma((8,)), dma((8,)),
            dma((2, 2, 4)), dma((2, 2, 4)), dma((2, 2, 4)), dma((2, 2, 4)), dma((2,)),
        ],
        compiler_params=pltpu.CompilerParams(
            collective_id=0, has_side_effects=True, vmem_limit_bytes=56 << 20
        ),
    )(bp, bu, pinv, uf, xs, ws)
    return pl.pallas_call(
        leave,
        name="leave",
        out_shape=outs,
        in_specs=[pl.BlockSpec(memory_space=vm)] * 3,
        out_specs=(pl.BlockSpec(memory_space=vm),) * 3,
    )(*results)


def solution(mesh):
    in_specs = (
        P("factor", "load"),
        P("factor", "load"),
        P("factor", None),
        P("factor", None),
        P(("factor", "load"), None),
        P("load", None),
    )
    out_specs = (P("factor", "load"), P("factor", "load"), P("load", "factor"))
    return jax.shard_map(local, mesh=mesh, in_specs=in_specs, out_specs=out_specs, check_vma=False)
```

```python
import functools

import jax
import jax.numpy as jnp
from jax import lax
from jax.experimental import pallas as pl
from jax.experimental.pallas import tpu as pltpu
from jax.sharding import PartitionSpec as P

MESH = pl.DeviceIdType.MESH
BF16 = jnp.bfloat16
F32 = jnp.float32
CHIPS = 8
ROWS = 128
COLS = 256


def kernel(
    bp, bu, pinv, uf, xs, ws, out_u, out_s, out_r,
    bp_all, f_all, red_all, p_v, pc, pt, u_v, ut, x_r, bu_v, w2, s_all,
    c_out, c_in, c_own, rs_out, rs_in, r_acc, r_in,
    loc, x_s, x_rv, ag_s, ag_r, sib_s, sib_r, p_s, p_r, w_s, w_r, c_s, c_r, rs_s, rs_r, fs, fr, ns, nr, r_s,
):
    f = lax.axis_index("factor")
    l = lax.axis_index("load")
    j, c = f // 2, f % 2
    h, y = j // 4, j % 4
    z, s = l // 2, l % 2
    sib = 2 * j + 1 - c

    pending = {}

    def settle(name):
        pending.pop(name)()

    def later(name, copy, lo, hi, how):
        def run():
            @pl.loop(lo, hi)
            def _(i):
                getattr(copy(i), how)()

        pending[name] = run

    def rdma(src, dst, ss, rs, df, dl):
        return pltpu.make_async_remote_copy(
            src_ref=src, dst_ref=dst, send_sem=ss, recv_sem=rs,
            device_id={"factor": df, "load": dl}, device_id_type=MESH,
        )

    def rows(ref, i, n=ROWS):
        return ref.at[pl.ds(pl.multiple_of(i * n, n), n)]

    def cols(ref, i, n):
        return ref.at[:, pl.ds(pl.multiple_of(i * n, n), n)]

    l_u = pltpu.make_async_copy(uf, u_v, loc.at[0])
    l_p = pltpu.make_async_copy(pinv, p_v, loc.at[1])
    l_b = pltpu.make_async_copy(bp, rows(bp_all, f), loc.at[2])
    l_x = pltpu.make_async_copy(cols(xs, l, COLS), rows(x_r, l, 16), loc.at[3])
    l_bu = pltpu.make_async_copy(bu, bu_v, loc.at[4])
    l_pc = pltpu.make_async_copy(cols(pinv, f, ROWS), pc.at[f], loc.at[5])
    for at, cp in enumerate((l_b, l_p, l_x, l_u, l_bu, l_pc)):
        cp.start()
        pending["l%d" % at] = cp.wait

    def l_w(i):
        return pltpu.make_async_copy(cols(ws, 2 * i + s, COLS), w2.at[i, pl.ds(0, 96)], loc.at[6 + i])

    @pl.loop(0, 16)
    def _(i):
        l_w(i).start()

    later("w own", l_w, 0, 16, "wait")

    barrier = pltpu.get_barrier_semaphore()

    def hello(df, dl):
        pl.semaphore_signal(barrier, inc=1, device_id={"factor": df, "load": dl}, device_id_type=MESH)

    @pl.loop(1, 32)
    def _(d):
        hello(f, (l + d) % 32)

    @pl.loop(1, 8)
    def _(d):
        hello(h * 8 + (f + d) % 8, l)

    @pl.loop(0, 8)
    def _(d):
        hello((1 - h) * 8 + d, 2 * z + 1 - s)

    @pl.loop(0, 4)
    def _(d):
        hello((1 - h) * 8 + 2 * d + c, l)

    pl.semaphore_wait(barrier, 31 + 7 + 8 + 4)

    def chip_copy(k, buf, d):
        own = rows(buf, f)
        return rdma(own, own, ag_s.at[k, d], ag_r.at[k, d], 2 * ((j + d) % CHIPS) + c, l)

    def chip_recv(k, buf, d):
        got = rows(buf, 2 * ((j + CHIPS - d) % CHIPS) + c)
        return rdma(got, got, ag_s.at[k, d], ag_r.at[k, d], sib, l)

    def core_copy(k, buf, d):
        got = rows(buf, 2 * ((j + CHIPS - d) % CHIPS) + c)
        return rdma(got, got, sib_s.at[k, d], sib_r.at[k, d], sib, l)

    def gather_start(k, buf):
        @pl.loop(1, CHIPS)
        def _(d):
            chip_copy(k, buf, d).start()

        core_copy(k, buf, 0).start()
        later(("chips sent", k), lambda d: chip_copy(k, buf, d), 1, CHIPS, "wait_send")
        later(("cores sent", k), lambda d: core_copy(k, buf, d), 0, CHIPS, "wait_send")
        later(("cores", k), lambda d: core_copy(k, buf, d), 0, CHIPS, "wait_recv")

    def gather_forward(k, buf):
        @pl.loop(1, CHIPS)
        def _(d):
            chip_recv(k, buf, d).wait_recv()
            core_copy(k, buf, d).start()

    def x_copy(d):
        to = (l + d) % 32
        return rdma(cols(xs, to, COLS), rows(x_r, l, 16), x_s.at[d], x_rv.at[d], f, to)

    def x_recv(d):
        got = rows(x_r, (l + 32 - d) % 32, 16)
        return rdma(got, got, x_s.at[d], x_rv.at[d], f, l)

    settle("l0")
    gather_start(0, bp_all)

    @pl.loop(1, 32)
    def _(d):
        x_copy(d).start()

    later("x sent", x_copy, 1, 32, "wait_send")
    later("x", x_recv, 1, 32, "wait_recv")

    def p_copy(d):
        to = (f + d) % 16
        same = 1 - (to // 8 + h) % 2
        dl = 2 * z + same * s + (1 - same) * (1 - s)
        return rdma(cols(p_v, to, ROWS), pc.at[f], p_s.at[d], p_r.at[d], to, dl)

    def p_recv(d):
        got = pc.at[(f + 16 - d) % 16]
        return rdma(got, got, p_s.at[d], p_r.at[d], sib, l)

    def w_copy(i):
        zz = 8 * c + i
        return rdma(
            cols(ws, 2 * zz + 1 - s, COLS), w2.at[zz, pl.ds(96, 96)], w_s.at[i], w_r.at[i], f, 2 * z + 1 - s
        )

    def w_core(i):
        got = w2.at[8 * c + i, pl.ds(96, 96)]
        return rdma(got, got, w_s.at[8 + i], w_r.at[8 + i], sib, l)

    def w_core_recv(i):
        got = w2.at[8 * (1 - c) + i, pl.ds(96, 96)]
        return rdma(got, got, w_s.at[8 + i], w_r.at[8 + i], sib, l)

    settle("l1")

    @pl.loop(1, 16)
    def _(d):
        p_copy(d).start()

    later("p sent", p_copy, 1, 16, "wait_send")
    later("p", p_recv, 1, 16, "wait_recv")

    @pl.loop(0, 8)
    def _(i):
        w_copy(i).start()

    later("w sent", w_copy, 0, 8, "wait_send")
    later("w", w_copy, 0, 8, "wait_recv")

    gather_forward(0, bp_all)

    settle(("cores", 0))
    fwd = jnp.dot(p_v[...], bp_all[...], preferred_element_type=F32).astype(BF16)
    f_all[pl.ds(pl.multiple_of(f * ROWS, ROWS), ROWS), :] = fwd

    settle("l3")

    @pl.loop(0, 16)
    def _(i):
        at = pl.ds(pl.multiple_of(i * ROWS, ROWS), ROWS)
        ut[at, :] = u_v[:, at].T

    settle("l2")

    settle("x")

    def c_copy(i):
        return rdma(c_out.at[i], c_in.at[i], c_s.at[i], c_r.at[i], sib, l)

    def partial(i, core):
        at = pl.ds(pl.multiple_of((2 * i + core) * ROWS, ROWS), ROWS)
        return jnp.dot(ut[at, :], x_r[...], preferred_element_type=F32)

    @pl.loop(1, CHIPS + 1)
    def _(d):
        i = (j + d) % CHIPS
        c_out[i] = partial(i, 1 - c).astype(BF16)
        c_copy(i).start()

    later("c sent", c_copy, 0, CHIPS, "wait_send")

    def rs_copy(d):
        to = (j + d) % CHIPS
        return rdma(rs_out.at[to], rs_in.at[d], rs_s.at[d], rs_r.at[d], 2 * to + c, l)

    @pl.loop(1, CHIPS)
    def _(d):
        to = (j + d) % CHIPS
        own = partial(to, c)
        c_copy(to).wait_recv()
        rs_out[to] = (own + c_in[to].astype(F32)).astype(BF16)
        rs_copy(d).start()

    later("rs sent", rs_copy, 1, CHIPS, "wait_send")
    c_own[...] = partial(j, c)
    c_copy(j).wait_recv()
    c_own[...] = c_own[...] + c_in[j].astype(F32)

    @pl.loop(1, CHIPS)
    def _(d):
        rs_copy(d).wait_recv()
        c_own[...] = c_own[...] + rs_in[d].astype(F32)

    mine = pl.ds(pl.multiple_of(f * ROWS, ROWS), ROWS)
    red_all[mine, :] = (f_all[mine, :].astype(F32) - c_own[...]).astype(BF16)
    gather_start(2, red_all)

    settle("l5")

    settle("p")

    @pl.loop(0, 16)
    def _(i):
        at = pl.ds(pl.multiple_of(i * ROWS, ROWS), ROWS)
        pt[:, at] = pc[i].T

    gather_forward(2, red_all)

    settle("w")

    @pl.loop(0, 8)
    def _(i):
        w_core(i).start()

    later("w core sent", w_core, 0, 8, "wait_send")
    later("w core", w_core_recv, 0, 8, "wait_recv")

    settle(("cores", 2))
    HALF = ROWS // 2
    legs = ((0, 1), (1, -1), (1, 1), (0, -1))

    def half(i, q):
        return s_all.at[i, pl.ds(q * HALF, HALF)]

    def last(q, way):
        return 4 if way == (1 - 2 * q) else 3

    def far(q, way, k):
        it = half((z + 32 - way * 2 * k) % 16, q)
        at = (q, (1 - way) // 2, k)
        return rdma(it, it, fs.at[at], fr.at[at], f, (l + 64 + 4 * way) % 32)

    def far_recv(q, way, k):
        it = half((z + 32 - way * (2 * k + 2)) % 16, q)
        at = (q, (1 - way) // 2, k)
        return rdma(it, it, fs.at[at], fr.at[at], sib, l)

    def near(q, way, k):
        it = half((z + 32 - way * 2 * k) % 16, q)
        at = (q, (1 - way) // 2, k)
        return rdma(it, it, ns.at[at], nr.at[at], f, (l + 64 + 2 * way) % 32)

    def near_recv(q, way, k):
        it = half((z + 32 - way * (2 * k + 1)) % 16, q)
        at = (q, (1 - way) // 2, k)
        return rdma(it, it, ns.at[at], nr.at[at], sib, l)

    def product(i):
        return lax.dot_general(w2[i % 16], s_all[i % 16], (((1,), (1,)), ((), ())), preferred_element_type=F32)

    for q in range(2):
        part = pl.ds(q * HALF, HALF)
        s_all[z, part, :] = jnp.dot(pt[part, :], red_all[...], preferred_element_type=F32).astype(BF16)
        for way in (1, -1):
            far(q, way, 0).start()
    for q, way in legs:
        near(q, way, 0).start()
        later(("far sent", q, way), lambda k, q=q, way=way: far(q, way, k), 0, last(q, way), "wait_send")
        later(("near sent", q, way), lambda k, q=q, way=way: near(q, way, k), 0, 4, "wait_send")
    gather_start(1, f_all)
    o_s = pltpu.make_async_copy(s_all.at[z], out_s, loc.at[23])
    o_s.start()
    settle("w own")
    settle("w core")
    r_acc[...] = product(z)
    for k in range(1, 4):
        for q, way in legs:
            far_recv(q, way, k - 1).wait_recv()
            if k < last(q, way):
                far(q, way, k).start()
        for q, way in legs:
            near(q, way, k).start()
        if k == 2:
            for name in (("chips sent", 0), ("cores sent", 0), "x sent", "p sent", "w sent", "c sent"):
                settle(name)
        if k == 3:
            for name in ("rs sent", "w core sent", ("chips sent", 2), ("cores sent", 2)):
                settle(name)
            gather_forward(1, f_all)
        r_acc[...] += product(z + 2 * k) + product(z + 16 - 2 * k)
        for q, way in legs:
            near_recv(q, way, k - 1).wait_recv()
        r_acc[...] += product(z + 2 * k - 1) + product(z + 17 - 2 * k)

    settle(("cores", 1))
    settle("l4")

    @pl.loop(0, 4)
    def _(i):
        at = pl.ds(pl.multiple_of(i * ROWS, ROWS), ROWS)
        low = jnp.dot(u_v[at, :], f_all[...], preferred_element_type=F32)
        bu_v[at, :] = (bu_v[at, :].astype(F32) - low).astype(BF16)

    o_u = pltpu.make_async_copy(bu_v, out_u, loc.at[22])
    o_u.start()

    for q, way in legs:
        near_recv(q, way, 3).wait_recv()
    r_acc[...] += product(z + 7) + product(z + 9)
    for q, way in legs[:2]:
        far_recv(q, way, 3).wait_recv()
    tail = product(z + 8)
    r_acc[pl.ds(96, 96), :] += tail[96:]
    swap = rdma(r_acc.at[pl.ds(96, 96)], r_in, r_s.at[0], r_s.at[1], f, 2 * z + 1 - s)
    swap.start()
    r_acc[pl.ds(0, 96), :] += tail[:96]

    for name in list(pending):
        settle(name)
    o_u.wait()
    o_s.wait()
    swap.wait()
    r_in[...] = r_acc[pl.ds(0, 96), :] + r_in[...]
    o_r = pltpu.make_async_copy(r_in, out_r, loc.at[24])
    o_r.start()
    o_r.wait()


def leave(u, s, r, out_u, out_s, out_r):
    out_u[...] = u[...]
    out_s[...] = s[...]
    out_r[...] = r[...]


def local(bp, bu, pinv, uf, xs, ws):
    dma = pltpu.SemaphoreType.DMA
    vm = pltpu.VMEM
    hbm = pl.BlockSpec(memory_space=pl.ANY)
    outs = (
        jax.ShapeDtypeStruct((512, COLS), BF16),
        jax.ShapeDtypeStruct((ROWS, COLS), BF16),
        jax.ShapeDtypeStruct((96, ROWS), F32),
    )
    results = pl.pallas_call(
        kernel,
        name="solves",
        out_shape=outs,
        in_specs=[hbm] * 6,
        out_specs=(hbm,) * 3,
        scratch_shapes=[
            vm((2048, COLS), BF16), vm((2048, COLS), BF16), vm((2048, COLS), BF16),
            vm((ROWS, 2048), BF16), vm((16, ROWS, ROWS), BF16), vm((ROWS, 2048), BF16),
            vm((512, 2048), BF16), vm((2048, 512), BF16), vm((512, COLS), BF16), vm((512, COLS), BF16),
            vm((16, 192, COLS), BF16), vm((16, ROWS, COLS), BF16),
            vm((CHIPS, ROWS, COLS), BF16), vm((CHIPS, ROWS, COLS), BF16), vm((ROWS, COLS), F32),
            vm((CHIPS, ROWS, COLS), BF16), vm((CHIPS, ROWS, COLS), BF16),
            vm((192, ROWS), F32), vm((96, ROWS), F32),
            dma((25,)), dma((32,)), dma((32,)), dma((3, 8)), dma((3, 8)), dma((3, 8)), dma((3, 8)),
            dma((16,)), dma((16,)), dma((16,)), dma((16,)), dma((8,)), dma((8,)), dma((8,)), dma((8,)),
            dma((2, 2, 4)), dma((2, 2, 4)), dma((2, 2, 4)), dma((2, 2, 4)), dma((2,)),
        ],
        compiler_params=pltpu.CompilerParams(
            collective_id=0, has_side_effects=True, vmem_limit_bytes=56 << 20
        ),
    )(bp, bu, pinv, uf, xs, ws)
    return pl.pallas_call(
        leave,
        name="leave",
        out_shape=outs,
        in_specs=[pl.BlockSpec(memory_space=vm)] * 3,
        out_specs=(pl.BlockSpec(memory_space=vm),) * 3,
    )(*results)


def solution(mesh):
    in_specs = (
        P("factor", "load"),
        P("factor", "load"),
        P("factor", None),
        P("factor", None),
        P(("factor", "load"), None),
        P("load", None),
    )
    out_specs = (P("factor", "load"), P("factor", "load"), P("load", "factor"))
    return jax.shard_map(local, mesh=mesh, in_specs=in_specs, out_specs=out_specs, check_vma=False)
```

```python
import functools

import jax
import jax.numpy as jnp
from jax import lax
from jax.experimental import pallas as pl
from jax.experimental.pallas import tpu as pltpu
from jax.sharding import PartitionSpec as P

MESH = pl.DeviceIdType.MESH
BF16 = jnp.bfloat16
F32 = jnp.float32
CHIPS = 8
ROWS = 128
COLS = 256


def kernel(
    bp, bu, pinv, uf, xs, ws, out_u, out_s, out_r,
    bp_all, f_all, red_all, p_v, pc, pt, u_v, ut, x_r, bu_v, w2, s_all,
    c_out, c_in, c_own, rs_out, rs_in, r_acc, r_in,
    loc, x_s, x_rv, ag_s, ag_r, sib_s, sib_r, p_s, p_r, w_s, w_r, c_s, c_r, rs_s, rs_r, fs, fr, ns, nr, r_s,
):
    f = lax.axis_index("factor")
    l = lax.axis_index("load")
    j, c = f // 2, f % 2
    h, y = j // 4, j % 4
    z, s = l // 2, l % 2
    sib = 2 * j + 1 - c

    pending = {}

    def settle(name):
        pending.pop(name)()

    def later(name, copy, lo, hi, how):
        def run():
            @pl.loop(lo, hi)
            def _(i):
                getattr(copy(i), how)()

        pending[name] = run

    def rdma(src, dst, ss, rs, df, dl):
        return pltpu.make_async_remote_copy(
            src_ref=src, dst_ref=dst, send_sem=ss, recv_sem=rs,
            device_id={"factor": df, "load": dl}, device_id_type=MESH,
        )

    def rows(ref, i, n=ROWS):
        return ref.at[pl.ds(pl.multiple_of(i * n, n), n)]

    def cols(ref, i, n):
        return ref.at[:, pl.ds(pl.multiple_of(i * n, n), n)]

    l_u = pltpu.make_async_copy(uf, u_v, loc.at[0])
    l_p = pltpu.make_async_copy(pinv, p_v, loc.at[1])
    l_b = pltpu.make_async_copy(bp, rows(bp_all, f), loc.at[2])
    l_x = pltpu.make_async_copy(cols(xs, l, COLS), rows(x_r, l, 16), loc.at[3])
    l_bu = pltpu.make_async_copy(bu, bu_v, loc.at[4])
    l_pc = pltpu.make_async_copy(cols(pinv, f, ROWS), pc.at[f], loc.at[5])
    for at, cp in enumerate((l_b, l_p, l_x, l_u, l_bu, l_pc)):
        cp.start()
        pending["l%d" % at] = cp.wait

    def l_w(i):
        return pltpu.make_async_copy(cols(ws, 2 * i + s, COLS), w2.at[i, pl.ds(0, 96)], loc.at[6 + i])

    @pl.loop(0, 16)
    def _(i):
        l_w(i).start()

    later("w own", l_w, 0, 16, "wait")

    barrier = pltpu.get_barrier_semaphore()

    def hello(df, dl):
        pl.semaphore_signal(barrier, inc=1, device_id={"factor": df, "load": dl}, device_id_type=MESH)

    @pl.loop(0, 31)
    def _(i):
        hello(f, (l + 16 + (i + 1) // 2 * (2 * (i % 2) - 1)) % 32)

    @pl.loop(1, 8)
    def _(d):
        hello(h * 8 + (f + d) % 8, l)

    @pl.loop(0, 8)
    def _(d):
        hello((1 - h) * 8 + d, 2 * z + 1 - s)

    @pl.loop(0, 4)
    def _(d):
        hello((1 - h) * 8 + 2 * d + c, l)

    pl.semaphore_wait(barrier, 31 + 7 + 8 + 4)

    def chip_copy(k, buf, d):
        own = rows(buf, f)
        return rdma(own, own, ag_s.at[k, d], ag_r.at[k, d], 2 * ((j + d) % CHIPS) + c, l)

    def chip_recv(k, buf, d):
        got = rows(buf, 2 * ((j + CHIPS - d) % CHIPS) + c)
        return rdma(got, got, ag_s.at[k, d], ag_r.at[k, d], sib, l)

    def core_copy(k, buf, d):
        got = rows(buf, 2 * ((j + CHIPS - d) % CHIPS) + c)
        return rdma(got, got, sib_s.at[k, d], sib_r.at[k, d], sib, l)

    def gather_start(k, buf):
        @pl.loop(1, CHIPS)
        def _(d):
            chip_copy(k, buf, d).start()

        core_copy(k, buf, 0).start()
        later(("chips sent", k), lambda d: chip_copy(k, buf, d), 1, CHIPS, "wait_send")
        later(("cores sent", k), lambda d: core_copy(k, buf, d), 0, CHIPS, "wait_send")
        later(("cores", k), lambda d: core_copy(k, buf, d), 0, CHIPS, "wait_recv")

    def gather_forward(k, buf):
        @pl.loop(1, CHIPS)
        def _(d):
            chip_recv(k, buf, d).wait_recv()
            core_copy(k, buf, d).start()

    def x_copy(d):
        to = (l + d) % 32
        return rdma(cols(xs, to, COLS), rows(x_r, l, 16), x_s.at[d], x_rv.at[d], f, to)

    def x_recv(d):
        got = rows(x_r, (l + 32 - d) % 32, 16)
        return rdma(got, got, x_s.at[d], x_rv.at[d], f, l)

    settle("l0")
    gather_start(0, bp_all)

    @pl.loop(1, 32)
    def _(d):
        x_copy(d).start()

    later("x sent", x_copy, 1, 32, "wait_send")
    later("x", x_recv, 1, 32, "wait_recv")

    def p_copy(d):
        to = (f + d) % 16
        same = 1 - (to // 8 + h) % 2
        dl = 2 * z + same * s + (1 - same) * (1 - s)
        return rdma(cols(p_v, to, ROWS), pc.at[f], p_s.at[d], p_r.at[d], to, dl)

    def p_recv(d):
        got = pc.at[(f + 16 - d) % 16]
        return rdma(got, got, p_s.at[d], p_r.at[d], sib, l)

    def w_copy(i):
        zz = 8 * c + i
        return rdma(
            cols(ws, 2 * zz + 1 - s, COLS), w2.at[zz, pl.ds(96, 96)], w_s.at[i], w_r.at[i], f, 2 * z + 1 - s
        )

    def w_core(i):
        got = w2.at[8 * c + i, pl.ds(96, 96)]
        return rdma(got, got, w_s.at[8 + i], w_r.at[8 + i], sib, l)

    def w_core_recv(i):
        got = w2.at[8 * (1 - c) + i, pl.ds(96, 96)]
        return rdma(got, got, w_s.at[8 + i], w_r.at[8 + i], sib, l)

    settle("l1")

    @pl.loop(1, 16)
    def _(d):
        p_copy(d).start()

    later("p sent", p_copy, 1, 16, "wait_send")
    later("p", p_recv, 1, 16, "wait_recv")

    @pl.loop(0, 8)
    def _(i):
        w_copy(i).start()

    later("w sent", w_copy, 0, 8, "wait_send")
    later("w", w_copy, 0, 8, "wait_recv")

    gather_forward(0, bp_all)

    settle(("cores", 0))
    fwd = jnp.dot(p_v[...], bp_all[...], preferred_element_type=F32).astype(BF16)
    f_all[pl.ds(pl.multiple_of(f * ROWS, ROWS), ROWS), :] = fwd

    settle("l3")

    @pl.loop(0, 16)
    def _(i):
        at = pl.ds(pl.multiple_of(i * ROWS, ROWS), ROWS)
        ut[at, :] = u_v[:, at].T

    settle("l2")

    settle("x")

    def c_copy(i):
        return rdma(c_out.at[i], c_in.at[i], c_s.at[i], c_r.at[i], sib, l)

    def partial(i, core):
        at = pl.ds(pl.multiple_of((2 * i + core) * ROWS, ROWS), ROWS)
        return jnp.dot(ut[at, :], x_r[...], preferred_element_type=F32)

    @pl.loop(0, CHIPS)
    def _(i):
        c_out[i] = partial(i, 1 - c).astype(BF16)
        c_copy(i).start()

    later("c sent", c_copy, 0, CHIPS, "wait_send")

    @pl.loop(0, CHIPS)
    def _(i):
        c_own[i] = partial(i, c)

    def rs_copy(d):
        to = (j + d) % CHIPS
        return rdma(rs_out.at[to], rs_in.at[d], rs_s.at[d], rs_r.at[d], 2 * to + c, l)

    @pl.loop(1, CHIPS)
    def _(d):
        to = (j + d) % CHIPS
        c_copy(to).wait_recv()
        rs_out[to] = (c_own[to] + c_in[to].astype(F32)).astype(BF16)
        rs_copy(d).start()

    later("rs sent", rs_copy, 1, CHIPS, "wait_send")
    c_copy(j).wait_recv()
    c_own[j] = c_own[j] + c_in[j].astype(F32)

    @pl.loop(1, CHIPS)
    def _(d):
        rs_copy(d).wait_recv()
        c_own[j] = c_own[j] + rs_in[d].astype(F32)

    mine = pl.ds(pl.multiple_of(f * ROWS, ROWS), ROWS)
    red_all[mine, :] = (f_all[mine, :].astype(F32) - c_own[j]).astype(BF16)
    gather_start(2, red_all)

    settle("l5")

    settle("p")

    @pl.loop(0, 16)
    def _(i):
        at = pl.ds(pl.multiple_of(i * ROWS, ROWS), ROWS)
        pt[:, at] = pc[i].T

    gather_forward(2, red_all)

    settle("w")

    @pl.loop(0, 8)
    def _(i):
        w_core(i).start()

    later("w core sent", w_core, 0, 8, "wait_send")
    later("w core", w_core_recv, 0, 8, "wait_recv")

    settle(("cores", 2))
    sol = jnp.dot(pt[...], red_all[...], preferred_element_type=F32).astype(BF16)
    s_all[z] = sol
    o_s = pltpu.make_async_copy(s_all.at[z], out_s, loc.at[23])
    o_s.start()

    HALF = ROWS // 2
    legs = ((0, 1), (1, -1), (1, 1), (0, -1))

    def half(i, q):
        return s_all.at[i, pl.ds(q * HALF, HALF)]

    def last(q, way):
        return 4 if way == (1 - 2 * q) else 3

    def far(q, way, k):
        it = half((z + 32 - way * 2 * k) % 16, q)
        at = (q, (1 - way) // 2, k)
        return rdma(it, it, fs.at[at], fr.at[at], f, (l + 64 + 4 * way) % 32)

    def far_recv(q, way, k):
        it = half((z + 32 - way * (2 * k + 2)) % 16, q)
        at = (q, (1 - way) // 2, k)
        return rdma(it, it, fs.at[at], fr.at[at], sib, l)

    def near(q, way, k):
        it = half((z + 32 - way * 2 * k) % 16, q)
        at = (q, (1 - way) // 2, k)
        return rdma(it, it, ns.at[at], nr.at[at], f, (l + 64 + 2 * way) % 32)

    def near_recv(q, way, k):
        it = half((z + 32 - way * (2 * k + 1)) % 16, q)
        at = (q, (1 - way) // 2, k)
        return rdma(it, it, ns.at[at], nr.at[at], sib, l)

    def product(i):
        return lax.dot_general(w2[i % 16], s_all[i % 16], (((1,), (1,)), ((), ())), preferred_element_type=F32)

    for q, way in legs:
        far(q, way, 0).start()
    for q, way in legs:
        near(q, way, 0).start()
        later(("far sent", q, way), lambda k, q=q, way=way: far(q, way, k), 0, last(q, way), "wait_send")
        later(("near sent", q, way), lambda k, q=q, way=way: near(q, way, k), 0, 4, "wait_send")
    gather_start(1, f_all)
    settle("w own")
    settle("w core")
    r_acc[...] = product(z)
    for k in range(1, 4):
        for q, way in legs:
            far_recv(q, way, k - 1).wait_recv()
            if k < last(q, way):
                far(q, way, k).start()
        for q, way in legs:
            near(q, way, k).start()
        if k == 3:
            gather_forward(1, f_all)
        r_acc[...] += product(z + 2 * k) + product(z + 16 - 2 * k)
        for q, way in legs:
            near_recv(q, way, k - 1).wait_recv()
        r_acc[...] += product(z + 2 * k - 1) + product(z + 17 - 2 * k)

    settle(("cores", 1))
    settle("l4")

    @pl.loop(0, 4)
    def _(i):
        at = pl.ds(pl.multiple_of(i * ROWS, ROWS), ROWS)
        low = jnp.dot(u_v[at, :], f_all[...], preferred_element_type=F32)
        bu_v[at, :] = (bu_v[at, :].astype(F32) - low).astype(BF16)

    o_u = pltpu.make_async_copy(bu_v, out_u, loc.at[22])
    o_u.start()

    for q, way in legs:
        near_recv(q, way, 3).wait_recv()
    r_acc[...] += product(z + 7) + product(z + 9)
    for q, way in legs[:2]:
        far_recv(q, way, 3).wait_recv()
    r_acc[...] += product(z + 8)

    swap = rdma(r_acc.at[pl.ds(96, 96)], r_in, r_s.at[0], r_s.at[1], f, 2 * z + 1 - s)
    swap.start()

    for name in list(pending):
        settle(name)
    o_u.wait()
    o_s.wait()
    swap.wait()
    r_in[...] = r_acc[pl.ds(0, 96), :] + r_in[...]
    o_r = pltpu.make_async_copy(r_in, out_r, loc.at[24])
    o_r.start()
    o_r.wait()


def leave(u, s, r, out_u, out_s, out_r):
    out_u[...] = u[...]
    out_s[...] = s[...]
    out_r[...] = r[...]


def local(bp, bu, pinv, uf, xs, ws):
    dma = pltpu.SemaphoreType.DMA
    vm = pltpu.VMEM
    hbm = pl.BlockSpec(memory_space=pl.ANY)
    outs = (
        jax.ShapeDtypeStruct((512, COLS), BF16),
        jax.ShapeDtypeStruct((ROWS, COLS), BF16),
        jax.ShapeDtypeStruct((96, ROWS), F32),
    )
    results = pl.pallas_call(
        kernel,
        name="solves",
        out_shape=outs,
        in_specs=[hbm] * 6,
        out_specs=(hbm,) * 3,
        scratch_shapes=[
            vm((2048, COLS), BF16), vm((2048, COLS), BF16), vm((2048, COLS), BF16),
            vm((ROWS, 2048), BF16), vm((16, ROWS, ROWS), BF16), vm((ROWS, 2048), BF16),
            vm((512, 2048), BF16), vm((2048, 512), BF16), vm((512, COLS), BF16), vm((512, COLS), BF16),
            vm((16, 192, COLS), BF16), vm((16, ROWS, COLS), BF16),
            vm((CHIPS, ROWS, COLS), BF16), vm((CHIPS, ROWS, COLS), BF16), vm((CHIPS, ROWS, COLS), F32),
            vm((CHIPS, ROWS, COLS), BF16), vm((CHIPS, ROWS, COLS), BF16),
            vm((192, ROWS), F32), vm((96, ROWS), F32),
            dma((25,)), dma((32,)), dma((32,)), dma((3, 8)), dma((3, 8)), dma((3, 8)), dma((3, 8)),
            dma((16,)), dma((16,)), dma((16,)), dma((16,)), dma((8,)), dma((8,)), dma((8,)), dma((8,)),
            dma((2, 2, 4)), dma((2, 2, 4)), dma((2, 2, 4)), dma((2, 2, 4)), dma((2,)),
        ],
        compiler_params=pltpu.CompilerParams(
            collective_id=0, has_side_effects=True, vmem_limit_bytes=56 << 20
        ),
    )(bp, bu, pinv, uf, xs, ws)
    return pl.pallas_call(
        leave,
        name="leave",
        out_shape=outs,
        in_specs=[pl.BlockSpec(memory_space=vm)] * 3,
        out_specs=(pl.BlockSpec(memory_space=vm),) * 3,
    )(*results)


def solution(mesh):
    in_specs = (
        P("factor", "load"),
        P("factor", "load"),
        P("factor", None),
        P("factor", None),
        P(("factor", "load"), None),
        P("load", None),
    )
    out_specs = (P("factor", "load"), P("factor", "load"), P("load", "factor"))
    return jax.shard_map(local, mesh=mesh, in_specs=in_specs, out_specs=out_specs, check_vma=False)
```
